256 devices in a mesh: sec: 8 (over y, core), proto: 32 (over z, x).
Axes of the slice: x: 4, y: 4, z: 8, core: 2. Of those that a mesh axis runs over, the one named last changes fastest.
Arguments:
- features: bfloat16 [4096, 512], P('sec'), may hold values from -700 to 700
- prototypes: bfloat16 [512, 262144], P(None, 'proto'), may hold values from -20 to 20
- crop_sample: int32 [4096], P('sec'), may hold values from 0 to 1023, as said below
- crop_live: int32 [4096], P('sec'), may hold values 0 or 1
Outputs:
- crop_loss: float32 [4096], P('sec')
- embed_grad: float32 [4096, 512], P(('sec', 'proto'))
The draws below stay inside these ranges and needn't reach their ends.
Inputs may be any that keep to these rules, and one draw needn't show every extreme that they name: `crop_sample`: on student rows the index of a teacher row, 0 to 1023; the entries on teacher rows are not read.
All inputs are finite; a program needn't handle non-finite values. No bound on the sum of `crop_live` on one device may be relied on, other than what follows from the above.
Results may differ from the reference program's by a relative error of at most 0.0067.
Values may be sent and summed in bfloat16 or wider, within the bound.
No kernel may reach another device: no remote copies, remote signals or barrier semaphores. Data moves between devices by JAX's collectives and lax.ppermute only.
A program may use at most 192 MiB of HBM per device.

```python
import math
import jax
import jax.numpy as jnp
from jax import lax

WIDTH = 512
PROTOS = 262144
ROWS_DEV = 512
ITERS = 3
SAMPLES = 1024
TEACH_FIRST = 1536
ALL_ROWS = 4096


def draw_features(key, part):
    keys = jax.random.split(jax.random.fold_in(key, 11), 3)
    drawn = jnp.clip(jax.random.normal(keys[0], (ALL_ROWS, WIDTH), jnp.float32), -6.0, 6.0)
    row_scale = jnp.exp(jax.random.uniform(keys[1], (ALL_ROWS, 1), jnp.float32, 0.0, math.log(10.0)))
    col_factor = jnp.exp(jax.random.uniform(keys[2], (1, WIDTH), jnp.float32, 0.0, math.log(10.0)))
    values = drawn * col_factor * row_scale
    return values.astype(jnp.bfloat16)


def draw_prototypes(key, part):
    noise_key = jax.random.fold_in(key, 13)
    values = jnp.clip(0.3 * jax.random.normal(noise_key, (WIDTH, PROTOS), jnp.float32), -1.8, 1.8)
    return values.astype(jnp.bfloat16)


def draw_crop_sample(key, part):
    picks = jax.random.randint(jax.random.fold_in(key, 17), (ALL_ROWS,), 0, SAMPLES, jnp.int32)
    return picks.at[0].set(SAMPLES - 1).at[1].set(0)


def set_ends(array, key, smallest, top_value):
    longest = array.shape.index(max(array.shape))
    spots = []
    for shift in (0, 1):
        where = [jax.random.randint(jax.random.fold_in(key, axis), (), 0, length) for axis, length in enumerate(array.shape)]
        where[longest] = (where[longest] + shift) % array.shape[longest]
        spots.append(tuple(where))
    return array.at[spots[0]].set(smallest).at[spots[1]].set(top_value)


def setup_inputs(seed: int = 0) -> dict:
    splits = jax.random.split(jax.random.key(seed), 5)
    features = draw_features(jax.random.fold_in(splits[4], 71), 0)
    prototypes = draw_prototypes(jax.random.fold_in(splits[4], 71), 0)
    crop_sample = draw_crop_sample(jax.random.fold_in(splits[4], 71), 0)
    crop_live = set_ends((jax.random.randint(splits[3], (ALL_ROWS,), 0, 4) < 3).astype(jnp.int32), jax.random.fold_in(splits[3], 1), 0, 1)
    return dict(features=features, prototypes=prototypes, crop_sample=crop_sample, crop_live=crop_live)


TEACH_TEMP = 0.07
STUD_TEMP = 0.1

def unit_rows_of(features):
    values = features.astype(jnp.float32)
    scaled = values * lax.rsqrt(lax.optimization_barrier(jnp.sum(values * values, axis=1, keepdims=True)) + 1e-06)
    return scaled.astype(jnp.bfloat16)

def reference(features, prototypes, crop_sample, crop_live):
    unit_rows = unit_rows_of(features)
    teach_end = TEACH_FIRST + SAMPLES
    teacher_logits = jnp.dot(unit_rows[TEACH_FIRST:teach_end], prototypes, preferred_element_type=jnp.float32) / TEACH_TEMP
    row_top = lax.optimization_barrier(jnp.max(teacher_logits, axis=1, keepdims=True))
    expo_tab = jnp.exp(teacher_logits - row_top)
    row_weight = jnp.ones((SAMPLES,), jnp.float32)
    col_scale = jnp.ones((PROTOS,), jnp.float32)
    for sweep in range(ITERS):
        col_scale = 1.0 / (PROTOS * jnp.dot(row_weight, expo_tab, precision=lax.Precision.HIGHEST))
        if sweep + 1 < ITERS:
            row_weight = 1.0 / (SAMPLES * jnp.dot(expo_tab, col_scale, precision=lax.Precision.HIGHEST))
    weighted = expo_tab * col_scale[None, :]
    targets = weighted / lax.optimization_barrier(jnp.sum(weighted, axis=1, keepdims=True))
    stud_all = jnp.concatenate([unit_rows[:TEACH_FIRST], unit_rows[teach_end:]], axis=0)
    index_all = jnp.concatenate([crop_sample[:TEACH_FIRST], crop_sample[teach_end:]], axis=0)
    live_all = jnp.concatenate([crop_live[:TEACH_FIRST], crop_live[teach_end:]], axis=0)
    stud_units = stud_all.reshape(-1, ROWS_DEV, WIDTH)
    stud_index = index_all.reshape(-1, ROWS_DEV).astype(jnp.int32)
    stud_live = live_all.reshape(-1, ROWS_DEV).astype(jnp.float32)

    def one_block(operands):
        unit_block, index_block, live_block = operands
        stud_logits = jnp.dot(unit_block, prototypes, preferred_element_type=jnp.float32) / STUD_TEMP
        stud_top = lax.optimization_barrier(jnp.max(stud_logits, axis=1, keepdims=True))
        log_total = stud_top[:, 0] + jnp.log(lax.optimization_barrier(jnp.sum(jnp.exp(stud_logits - stud_top), axis=1)))
        stud_probs = jnp.exp(stud_logits - log_total[:, None])
        chosen = jnp.take(targets, index_block, axis=0)
        loss_block = live_block * (log_total - lax.optimization_barrier(jnp.sum(chosen * stud_logits, axis=1)))
        prob_gap = (live_block[:, None] * (stud_probs - chosen)).astype(jnp.bfloat16)
        grad_block = lax.dot_general(prob_gap, prototypes, (((1,), (1,)), ((), ())), preferred_element_type=jnp.float32) / STUD_TEMP
        return (loss_block, grad_block)
    losses, grads = lax.map(one_block, (stud_units, stud_index, stud_live))
    losses = losses.reshape(-1)
    grads = grads.reshape(-1, WIDTH)
    crop_loss = jnp.concatenate([losses[:TEACH_FIRST], jnp.zeros((SAMPLES,), jnp.float32), losses[TEACH_FIRST:]], axis=0)
    embed_grad = jnp.concatenate([grads[:TEACH_FIRST], jnp.zeros((SAMPLES, WIDTH), jnp.float32), grads[TEACH_FIRST:]], axis=0)
    return (crop_loss, embed_grad)
```

```python
import functools

import jax
import jax.numpy as jnp
from jax import lax
from jax.experimental import pallas as pl
from jax.experimental.pallas import tpu as pltpu
from jax.sharding import PartitionSpec as P

PROTOS = 262144
SAMPLES = 1024
TEACH_TEMP = 0.07
STUD_TEMP = 0.1

F32 = jnp.float32
BF16 = jnp.bfloat16
LANES = 128
SUBS = 8

TEACH_A = 3
TEACH_B = 4

def is_teacher():
    sec = lax.axis_index("sec")
    return jnp.logical_or(sec == TEACH_A, sec == TEACH_B)


def row_to_column(row):
    return jnp.transpose(jnp.broadcast_to(row, (LANES, row.shape[1])))


def lanes_to_row(acc, reduce):
    return reduce(jnp.transpose(acc), axis=0, keepdims=True)


def pack_row(row):
    return jnp.concatenate(
        [row[:, i * LANES : (i + 1) * LANES] for i in range(row.shape[1] // LANES)], axis=0
    )


def unpack_row(packed):
    return jnp.concatenate([packed[i : i + 1, :] for i in range(packed.shape[0])], axis=1)


def tile_lanes(column, count):
    return jnp.concatenate([column] * count, axis=1)


def split_high(x):
    high = x.astype(BF16).astype(F32)
    return high, x - high


def write_parts(send_ref, product, rows):
    parts, each, _ = send_ref.shape
    width = product.shape[1]
    send_ref[:, :, :width] = product.astype(BF16).reshape(parts, each, width)
    extra = jnp.concatenate(rows, axis=0).astype(BF16)
    send_ref[:, :, width:] = jnp.broadcast_to(extra[None], (parts, each, LANES))


def send_copies(ref, packed):
    ref[...] = jnp.broadcast_to(packed[None], ref.shape)


def fold_lanes(op, block):
    out = block[:, :LANES]
    for i in range(1, block.shape[1] // LANES):
        out = op(out, block[:, i * LANES : (i + 1) * LANES])
    return out


def start_stream(w_hbm, w_ref, sems):
    chunk = w_ref.shape[1] // sems.shape[0]
    for j in range(sems.shape[0]):
        at = pl.ds(j * chunk, chunk)
        pltpu.make_async_copy(w_hbm.at[:, at], w_ref.at[:, at], sems.at[j]).start()


def wait_stream(w_hbm, w_ref, sems, j):
    chunk = w_ref.shape[1] // sems.shape[0]
    at = pl.ds(pl.multiple_of(j * chunk, chunk), chunk)
    pltpu.make_async_copy(w_hbm.at[:, at], w_ref.at[:, at], sems.at[j]).wait()


def unit_rows(features):
    values = features.astype(F32)
    total = jnp.sum(values * values, axis=1, keepdims=True)
    return (values * lax.rsqrt(total + 1e-06)).astype(BF16)


def logits_into(lhs_ref, w_ref, out_ref, top_ref, scale, wait=None, chunk=512):
    cols = w_ref.shape[1]
    top_ref[...] = jnp.full(top_ref.shape, -jnp.inf, F32)

    def step(j, carry):
        if wait is not None:
            wait(j)
        at = pl.ds(pl.multiple_of(j * chunk, chunk), chunk)
        z = jnp.dot(lhs_ref[...], w_ref[:, at], preferred_element_type=F32) * scale
        out_ref[:, at] = z
        top_ref[...] = jnp.maximum(top_ref[...], fold_lanes(jnp.maximum, z))
        return carry

    lax.fori_loop(0, cols // chunk, step, 0)


def column_sums(e_ref, weight_ref, put, width=512, block=64):
    rows, cols = e_ref.shape

    def step(j, carry):
        at = pl.ds(pl.multiple_of(j * width, width), width)

        def inner(i, acc):
            r = pl.ds(pl.multiple_of(i * block, block), block)
            x = e_ref[r, at] * tile_lanes(weight_ref[r, :], width // LANES)
            return acc + jnp.sum(x.reshape(block // SUBS, SUBS, width), axis=0)

        acc = lax.fori_loop(0, rows // block, inner, jnp.zeros((SUBS, width), F32))
        put(at, jnp.sum(acc, axis=0, keepdims=True))
        return carry

    lax.fori_loop(0, cols // width, step, 0)


def row_sums(e_ref, scale_ref, acc_ref, block=64, width=1024):
    rows, cols = e_ref.shape

    def step(i, carry):
        r = pl.ds(pl.multiple_of(i * block, block), block)

        def inner(j, acc):
            at = pl.ds(pl.multiple_of(j * width, width), width)
            x = e_ref[r, at] * scale_ref[:, at]
            return acc + fold_lanes(jnp.add, x)

        acc_ref[r, :] = lax.fori_loop(0, cols // width, inner, jnp.zeros((block, LANES), F32))
        return carry

    lax.fori_loop(0, rows // block, step, 0)


def first_logits(x_ref, w_hbm, l_ref, u_ref, send_ref, top_ref, w_ref, sems, *, scale):
    start_stream(w_hbm, w_ref, sems)
    u_ref[...] = unit_rows(x_ref[...])

    def wait(j):
        wait_stream(w_hbm, w_ref, sems, j)

    logits_into(u_ref, w_ref, l_ref, top_ref, scale, wait)
    packed = pack_row(lanes_to_row(top_ref[...], jnp.max))
    if len(send_ref.shape) == 3:
        send_copies(send_ref, packed)
    else:
        send_ref[...] = packed


def teacher_exponentials(l_ref, got_ref, e_ref, col_ref, top_ref, *, width=512, block=64):
    top_ref[...] = row_to_column(unpack_row(jnp.max(got_ref[...], axis=0)))
    rows, cols = e_ref.shape

    def step(j, carry):
        at = pl.ds(pl.multiple_of(j * width, width), width)

        def inner(i, acc):
            r = pl.ds(pl.multiple_of(i * block, block), block)
            x = jnp.exp(l_ref[r, at] - tile_lanes(top_ref[r, :], width // LANES))
            e_ref[r, at] = x
            return acc + jnp.sum(x.reshape(block // SUBS, SUBS, width), axis=0)

        acc = lax.fori_loop(0, rows // block, inner, jnp.zeros((SUBS, width), F32))
        col_ref[:, at] = jnp.sum(acc, axis=0, keepdims=True)
        return carry

    lax.fori_loop(0, cols // width, step, 0)


def teacher_rows(e_ref, own_ref, peer_ref, send_ref, scale_ref, acc_ref):
    scale_ref[...] = 1.0 / (PROTOS * (own_ref[...] + peer_ref[...]))
    row_sums(e_ref, scale_ref, acc_ref)
    send_copies(send_ref, pack_row(lanes_to_row(acc_ref[...], jnp.sum)))


def teacher_columns(e_ref, got_ref, col_ref, weight_ref):
    total = unpack_row(jnp.sum(got_ref[...], axis=0))
    weight_ref[...] = row_to_column(1.0 / (SAMPLES * total))

    def put(at, sums):
        col_ref[:, at] = sums

    column_sums(e_ref, weight_ref, put)


def teacher_last(e_ref, got_ref, top_ref, col_ref, weight_ref):
    total = unpack_row(jnp.sum(got_ref[...], axis=0))
    weight_ref[...] = row_to_column(1.0 / (SAMPLES * total))
    top = unpack_row(jnp.max(top_ref[...], axis=0))

    def put(at, sums):
        for s in range(col_ref.shape[0]):
            col_ref[s, :, at] = sums

    column_sums(e_ref, weight_ref, put)
    for s in range(col_ref.shape[0]):
        col_ref[s, :, e_ref.shape[1] :] = top


def student_product(
    l_ref, top_ref, w_hbm, send_ref, acc_ref, sum_ref, w_ref, sems
):
    start_stream(w_hbm, w_ref, sems)
    chunk = w_ref.shape[1] // sems.shape[0]
    packed = top_ref[...].astype(BF16).astype(F32)
    top = row_to_column(unpack_row(packed))
    acc_ref[...] = jnp.zeros_like(acc_ref)
    sum_ref[...] = jnp.zeros_like(sum_ref)

    def step(j, carry):
        at = pl.ds(pl.multiple_of(j * chunk, chunk), chunk)
        x = jnp.exp(l_ref[:, at] - tile_lanes(top, chunk // LANES))
        sum_ref[...] += fold_lanes(jnp.add, x)
        wait_stream(w_hbm, w_ref, sems, j)
        acc_ref[...] += lax.dot_general(
            x.astype(BF16), w_ref[:, at], (((1,), (1,)), ((), ())), preferred_element_type=F32
        )
        return carry

    lax.fori_loop(0, sems.shape[0], step, 0)
    high, low = split_high(pack_row(lanes_to_row(sum_ref[...], jnp.sum)))
    write_parts(send_ref, acc_ref[...], [packed, high, low, jnp.zeros_like(low)])


def stack_rows(p1_ref, p2_ref, both_ref):
    low = lax.axis_index("sec") < lax.axis_size("sec") // 2
    half = p1_ref.shape[0]

    @pl.when(low)
    def _():
        both_ref[:half, :] = p1_ref[...]
        both_ref[half:, :] = p2_ref[...]

    @pl.when(jnp.logical_not(low))
    def _():
        both_ref[:half, :] = p2_ref[...]
        both_ref[half:, :] = p1_ref[...]


def crop_first(
    w_hbm, index_ref, both_ref, p3_ref, p4_ref, ec_ref, send_ref, top_ref, crop_ref, rows_ref,
    w_ref, lc_ref, sems,
):
    start_stream(w_hbm, w_ref, sems)
    sec = lax.axis_index("sec")

    @pl.when(jnp.logical_or(sec == 2, sec == 5))
    def _():
        rows_ref[...] = both_ref[...]

    @pl.when(jnp.logical_or(sec == 0, sec == 7))
    def _():
        rows_ref[...] = p3_ref[...]

    @pl.when(jnp.logical_or(sec == 1, sec == 6))
    def _():
        rows_ref[...] = p4_ref[...]

    index = row_to_column(unpack_row(index_ref[...]))
    picked = jnp.zeros(crop_ref.shape, F32)
    for start in range(0, rows_ref.shape[0], 512):
        lane = lax.broadcasted_iota(jnp.int32, (index.shape[0], 512), 1) + start
        hot = jnp.where(tile_lanes(index, 4) == lane, 1.0, 0.0).astype(BF16)
        picked += jnp.dot(hot, rows_ref[start : start + 512, :], preferred_element_type=F32)
    crop_ref[...] = unit_rows(picked)

    def wait(j):
        wait_stream(w_hbm, w_ref, sems, j)

    logits_into(crop_ref, w_ref, lc_ref, top_ref, 1.0 / TEACH_TEMP, wait)
    row = lanes_to_row(top_ref[...], jnp.max)
    send_ref[...] = pack_row(row)
    top_ref[...] = row_to_column(row)
    width, block = 512, 64

    def outer(j, carry):
        at = pl.ds(pl.multiple_of(j * width, width), width)

        def inner(i, carry):
            r = pl.ds(pl.multiple_of(i * block, block), block)
            x = jnp.exp(lc_ref[r, at] - tile_lanes(top_ref[r, :], width // LANES))
            ec_ref[r, at] = x.astype(BF16)
            return carry

        return lax.fori_loop(0, lc_ref.shape[0] // block, inner, carry)

    lax.fori_loop(0, lc_ref.shape[1] // width, outer, 0)


def crop_product(
    ec_ref, cols_ref, w_ref, u_ref, index_ref, top_ref, send_ref, c_ref, acc_ref, fix_ref,
    *, chunk=1024,
):
    rows, cols = ec_ref.shape
    index = row_to_column(unpack_row(index_ref[...]))
    lane = lax.broadcasted_iota(jnp.int32, index.shape, 1)
    picked = jnp.zeros(index.shape, F32)
    for s, owner in enumerate((TEACH_A, TEACH_B)):
        for t in range(rows // LANES):
            tops = cols_ref[owner, :, cols + t * LANES : cols + (t + 1) * LANES]
            picked = jnp.where(index == lane + (s * rows + t * LANES), tops, picked)
    picked = jnp.sum(picked, axis=1, keepdims=True)
    fix_ref[...] = jnp.exp(row_to_column(unpack_row(top_ref[...])) - picked)
    c_ref[...] = jnp.zeros_like(c_ref)
    acc_ref[...] = jnp.zeros_like(acc_ref)

    def step(j, carry):
        at = pl.ds(pl.multiple_of(j * chunk, chunk), chunk)
        scale = 1.0 / (PROTOS * (cols_ref[TEACH_A, :, at] + cols_ref[TEACH_B, :, at]))
        y = ec_ref[:, at].astype(F32) * tile_lanes(fix_ref[...], chunk // LANES) * scale
        acc_ref[...] += fold_lanes(jnp.add, y)
        c_ref[...] += lax.dot_general(
            y.astype(BF16), w_ref[:, at], (((1,), (1,)), ((), ())), preferred_element_type=F32
        )
        return carry

    lax.fori_loop(0, cols // chunk, step, 0)
    cross = fold_lanes(jnp.add, u_ref[...].astype(F32) * c_ref[...]) * (1.0 / STUD_TEMP)
    total = split_high(pack_row(lanes_to_row(acc_ref[...], jnp.sum)))
    cross = split_high(pack_row(lanes_to_row(cross, jnp.sum)))
    write_parts(send_ref, c_ref[...], [*total, *cross])


def finish(a_ref, c_ref, live_ref, grad_ref, loss_ref, weight_ref, stud_ref, targ_ref):
    each, width = grad_ref.shape
    packs = live_ref.shape[0]
    teacher = is_teacher()

    @pl.when(teacher)
    def _():
        grad_ref[...] = jnp.zeros_like(grad_ref)
        loss_ref[...] = jnp.zeros_like(loss_ref)

    @pl.when(jnp.logical_not(teacher))
    def _():
        parts = a_ref.shape[0]
        extra = a_ref[:, :, width:].astype(F32)
        tops = extra[:, :packs]
        top = jnp.max(tops, axis=0)
        weight = jnp.exp(tops - top[None])
        sums = extra[:, packs : 2 * packs] + extra[:, 2 * packs : 3 * packs]
        total = jnp.sum(weight * sums, axis=0)
        rest = jnp.zeros((LANES - parts, LANES), F32)
        for i in range(packs):
            piece = jnp.concatenate([weight[:, i, :], rest], axis=0)
            weight_ref[i * LANES : (i + 1) * LANES, :] = jnp.transpose(piece)
        extra = jnp.sum(c_ref[:, :, width:].astype(F32), axis=0)
        target_sum = extra[:packs] + extra[packs : 2 * packs]
        cross = extra[2 * packs : 3 * packs] + extra[3 * packs :]
        live = live_ref[...].astype(F32)
        loss_ref[...] = live * (top + jnp.log(total) - cross / target_sum)
        scale = live * (1.0 / STUD_TEMP)
        stud_ref[...] = row_to_column(unpack_row(scale / total))
        targ_ref[...] = row_to_column(unpack_row(scale / target_sum))
        mine = pl.ds(pl.multiple_of(lax.axis_index("proto") * each, each), each)
        tiles = width // LANES
        factor = weight_ref[mine, :]
        stud = jnp.zeros(grad_ref.shape, F32)
        for p in range(parts):
            stud += a_ref[p, :, :width].astype(F32) * factor[:, p : p + 1]
        targ = jnp.sum(c_ref[:, :, :width].astype(F32), axis=0)
        grad_ref[...] = stud * tile_lanes(stud_ref[mine, :], tiles) - targ * tile_lanes(
            targ_ref[mine, :], tiles
        )


def relay(x_ref, y_ref):
    y_ref[...] = x_ref[...]


def hollow(*refs):
    pass


MIB = 2**20
HBM = pltpu.HBM
VMEM = pltpu.VMEM


def call(
    kernel, out, args, scratch=(), alias=None, flops=0, moved=0, limit=8, spaces=None, name=None,
    out_space=VMEM,
):
    spaces = spaces or [VMEM] * len(args)
    return pl.pallas_call(
        kernel,
        name=name or kernel.__name__,
        out_shape=tuple(jax.ShapeDtypeStruct(s, d) for s, d in out),
        in_specs=[pl.BlockSpec(memory_space=s) for s in spaces],
        out_specs=tuple([pl.BlockSpec(memory_space=out_space)] * len(out)),
        scratch_shapes=list(scratch),
        input_output_aliases=alias or {},
        cost_estimate=pl.CostEstimate(flops=flops, bytes_accessed=moved, transcendentals=0),
        compiler_params=pltpu.CompilerParams(vmem_limit_bytes=limit * MIB),
    )(*args)


def per_device(features, prototypes, crop_sample, crop_live):
    rows, width = features.shape
    cols = prototypes.shape[1]
    protos = lax.axis_size("proto")
    secs = lax.axis_size("sec")
    packs = rows // LANES
    each = rows // protos
    row_send = ((protos, packs, LANES), F32)
    one_row = ((packs, LANES), F32)
    parts = ((protos, each, width + LANES), BF16)
    column = ((1, cols), F32)
    columns = ((secs, 1, cols + rows), F32)
    table = ((rows, cols), F32)
    crop_table = ((rows, cols), BF16)
    units = ((rows, width), BF16)
    both_rows = ((2 * rows, width), BF16)
    lanes = VMEM((rows, LANES), F32)
    product = VMEM((rows, width), F32)
    line = VMEM((1, cols), F32)
    protos_vmem = VMEM((width, cols), BF16)
    big = rows * cols * 4
    gemm = 2 * rows * cols * width
    index = crop_sample.reshape(packs, LANES)
    live = crop_live.reshape(packs, LANES)
    pair = [(TEACH_A, TEACH_B), (TEACH_B, TEACH_A)]

    def sems(count):
        return pltpu.SemaphoreType.DMA((count,))

    def spread(x):
        return lax.all_to_all(x, "proto", 0, 0, tiled=True)

    def unused(after, *out):
        return call(hollow, out, [after], spaces=[pl.ANY], out_space=pl.ANY)

    def start(temp, send):
        return call(
            functools.partial(first_logits, scale=1.0 / temp),
            [table, units, send],
            [features, prototypes],
            [lanes, protos_vmem, sems(16)],
            flops=gemm, moved=big, spaces=[VMEM, HBM], limit=32, name="first_logits",
        )

    def teacher(p1):
        logits, _, send = start(TEACH_TEMP, row_send)
        top_got = spread(send)
        expo, col = call(
            teacher_exponentials, [table, column], [logits, top_got], [lanes], {0: 0},
            flops=big, moved=big,
        )
        for last in (False, True):
            peer = lax.ppermute(col, "sec", pair)
            (send,) = call(
                teacher_rows, [row_send], [expo, col, peer], [line, lanes], flops=big, moved=big
            )
            got = spread(send)
            if last:
                (col,) = call(
                    teacher_last, [columns], [expo, got, top_got], [lanes], flops=big, moved=big
                )
            else:
                (col,) = call(
                    teacher_columns, [column], [expo, got], [lanes], flops=big, moved=big
                )
        return col, *unused(col, crop_table, units, one_row, parts)

    def student(p1):
        p2 = lax.ppermute(p1, "sec", [(2, 5), (5, 2)])
        logits, unit, top = start(STUD_TEMP, one_row)
        top, p2 = lax.optimization_barrier((top, p2))
        (both,) = call(stack_rows, [both_rows], [p1, p2])
        p3 = lax.ppermute(both, "sec", [(2, 0), (5, 7)])
        (send,) = call(
            student_product, [parts], [logits, top, prototypes],
            [product, lanes, protos_vmem, sems(8)],
            flops=gemm, moved=big, spaces=[VMEM, VMEM, HBM], limit=32,
        )
        stud_got = spread(send)
        p3, stud_got = lax.optimization_barrier((p3, stud_got))
        p4 = lax.ppermute(p3, "sec", [(0, 1), (7, 6)])
        crop_expo, crop_top = call(
            crop_first,
            [crop_table, one_row],
            [prototypes, index, both, p3, p4],
            [lanes, VMEM(units[0], BF16), VMEM(both_rows[0], BF16), protos_vmem, VMEM(*table), sems(16)],
            flops=gemm, moved=big, spaces=[HBM] + [VMEM] * 4, limit=48,
        )
        return *unused(crop_expo, columns), crop_expo, unit, crop_top, stud_got

    p1 = lax.ppermute(features, "sec", [(3, 2), (4, 5)])
    col, expo, unit, crop_top, stud_got = lax.cond(is_teacher(), teacher, student, p1)
    (col,) = call(relay, [columns], [col], flops=gemm, moved=big)
    cols_got = lax.all_to_all(col, "sec", 0, 0, tiled=True)
    (send,) = call(
        crop_product,
        [parts],
        [expo, cols_got, prototypes, unit, index, crop_top],
        [product, lanes, lanes],
        flops=gemm, moved=big, limit=12,
    )
    grad, loss = call(
        finish,
        [((each, width), F32), ((packs, LANES), F32)],
        [stud_got, spread(send), live],
        [lanes, lanes, lanes],
    )
    return loss.reshape(rows), grad


def solution(mesh):
    in_specs = (P("sec", None), P(None, "proto"), P("sec"), P("sec"))
    out_specs = (P("sec"), P(("sec", "proto"), None))
    return jax.shard_map(
        per_device, mesh=mesh, in_specs=in_specs, out_specs=out_specs, check_vma=False
    )
```

```python
import functools

import jax
import jax.numpy as jnp
from jax import lax
from jax.experimental import pallas as pl
from jax.experimental.pallas import tpu as pltpu
from jax.sharding import PartitionSpec as P

PROTOS = 262144
SAMPLES = 1024
TEACH_TEMP = 0.07
STUD_TEMP = 0.1

F32 = jnp.float32
BF16 = jnp.bfloat16
LANES = 128
SUBS = 8

TEACH_A = 3
TEACH_B = 4

def is_teacher():
    sec = lax.axis_index("sec")
    return jnp.logical_or(sec == TEACH_A, sec == TEACH_B)


def row_to_column(row):
    return jnp.transpose(jnp.broadcast_to(row, (LANES, row.shape[1])))


def lanes_to_row(acc, reduce):
    return reduce(jnp.transpose(acc), axis=0, keepdims=True)


def pack_row(row):
    return jnp.concatenate(
        [row[:, i * LANES : (i + 1) * LANES] for i in range(row.shape[1] // LANES)], axis=0
    )


def unpack_row(packed):
    return jnp.concatenate([packed[i : i + 1, :] for i in range(packed.shape[0])], axis=1)


def tile_lanes(column, count):
    return jnp.concatenate([column] * count, axis=1)


def split_high(x):
    high = x.astype(BF16).astype(F32)
    return high, x - high


def write_parts(send_ref, product, rows):
    parts, each, _ = send_ref.shape
    width = product.shape[1]
    send_ref[:, :, :width] = product.astype(BF16).reshape(parts, each, width)
    extra = jnp.concatenate(rows, axis=0).astype(BF16)
    send_ref[:, :, width:] = jnp.broadcast_to(extra[None], (parts, each, LANES))


def send_copies(ref, packed):
    ref[...] = jnp.broadcast_to(packed[None], ref.shape)


def fold_lanes(op, block):
    out = block[:, :LANES]
    for i in range(1, block.shape[1] // LANES):
        out = op(out, block[:, i * LANES : (i + 1) * LANES])
    return out


def block_copy(w_hbm, w_ref, sems, j):
    chunk = w_ref.shape[1] // sems.shape[0]
    at = pl.ds(pl.multiple_of(j * chunk, chunk), chunk)
    return pltpu.make_async_copy(w_hbm.at[:, at], w_ref.at[:, at], sems.at[j])


def start_stream(w_hbm, w_ref, sems):
    block_copy(w_hbm, w_ref, sems, 0).start()


def wait_stream(w_hbm, w_ref, sems, j):
    block_copy(w_hbm, w_ref, sems, j).wait()

    @pl.when(j + 1 < sems.shape[0])
    def _():
        block_copy(w_hbm, w_ref, sems, j + 1).start()


def unit_rows(features):
    values = features.astype(F32)
    total = jnp.sum(values * values, axis=1, keepdims=True)
    return (values * lax.rsqrt(total + 1e-06)).astype(BF16)


def logits_into(lhs_ref, w_ref, out_ref, top_ref, scale, wait, chunk):
    cols = w_ref.shape[1]
    top_ref[...] = jnp.full(top_ref.shape, -jnp.inf, F32)

    def step(j, carry):
        wait(j)
        at = pl.ds(pl.multiple_of(j * chunk, chunk), chunk)
        z = jnp.dot(lhs_ref[...], w_ref[:, at], preferred_element_type=F32) * scale
        out_ref[:, at] = z
        top_ref[...] = jnp.maximum(top_ref[...], fold_lanes(jnp.maximum, z))
        return carry

    lax.fori_loop(0, cols // chunk, step, 0)


def column_sums(e_ref, weight_ref, put, width=512, block=256):
    rows, cols = e_ref.shape

    def step(j, carry):
        at = pl.ds(pl.multiple_of(j * width, width), width)

        def inner(i, acc):
            r = pl.ds(pl.multiple_of(i * block, block), block)
            x = e_ref[r, at] * tile_lanes(weight_ref[r, :], width // LANES)
            return acc + jnp.sum(x.reshape(block // SUBS, SUBS, width), axis=0)

        acc = lax.fori_loop(0, rows // block, inner, jnp.zeros((SUBS, width), F32))
        put(at, jnp.sum(acc, axis=0, keepdims=True))
        return carry

    lax.fori_loop(0, cols // width, step, 0)


def row_sums(e_ref, scale_ref, acc_ref, block=64, width=1024):
    rows, cols = e_ref.shape

    def step(i, carry):
        r = pl.ds(pl.multiple_of(i * block, block), block)

        def inner(j, acc):
            at = pl.ds(pl.multiple_of(j * width, width), width)
            x = e_ref[r, at] * scale_ref[:, at]
            return acc + fold_lanes(jnp.add, x)

        acc_ref[r, :] = lax.fori_loop(0, cols // width, inner, jnp.zeros((block, LANES), F32))
        return carry

    lax.fori_loop(0, rows // block, step, 0)


def first_logits(x_ref, w_hbm, l_ref, u_ref, send_ref, top_ref, w_ref, sems, *, scale):
    start_stream(w_hbm, w_ref, sems)
    u_ref[...] = unit_rows(x_ref[...])

    def wait(j):
        wait_stream(w_hbm, w_ref, sems, j)

    logits_into(u_ref, w_ref, l_ref, top_ref, scale, wait, w_ref.shape[1] // sems.shape[0])
    packed = pack_row(lanes_to_row(top_ref[...], jnp.max))
    if len(send_ref.shape) == 3:
        send_copies(send_ref, packed)
    else:
        send_ref[...] = packed


def teacher_exponentials(l_ref, got_ref, e_ref, col_ref, top_ref, *, width=512, block=256):
    top_ref[...] = row_to_column(unpack_row(jnp.max(got_ref[...], axis=0)))
    rows, cols = e_ref.shape

    def step(j, carry):
        at = pl.ds(pl.multiple_of(j * width, width), width)

        def inner(i, acc):
            r = pl.ds(pl.multiple_of(i * block, block), block)
            x = jnp.exp(l_ref[r, at] - tile_lanes(top_ref[r, :], width // LANES))
            e_ref[r, at] = x
            return acc + jnp.sum(x.reshape(block // SUBS, SUBS, width), axis=0)

        acc = lax.fori_loop(0, rows // block, inner, jnp.zeros((SUBS, width), F32))
        col_ref[:, at] = jnp.sum(acc, axis=0, keepdims=True)
        return carry

    lax.fori_loop(0, cols // width, step, 0)


def teacher_rows(e_ref, own_ref, peer_ref, send_ref, scale_ref, acc_ref):
    scale_ref[...] = 1.0 / (PROTOS * (own_ref[...] + peer_ref[...]))
    row_sums(e_ref, scale_ref, acc_ref)
    send_copies(send_ref, pack_row(lanes_to_row(acc_ref[...], jnp.sum)))


def teacher_columns(e_ref, got_ref, col_ref, weight_ref):
    total = unpack_row(jnp.sum(got_ref[...], axis=0))
    weight_ref[...] = row_to_column(1.0 / (SAMPLES * total))

    def put(at, sums):
        col_ref[:, at] = sums

    column_sums(e_ref, weight_ref, put)


def teacher_last(e_ref, got_ref, top_ref, col_ref, weight_ref, line_ref):
    total = unpack_row(jnp.sum(got_ref[...], axis=0))
    weight_ref[...] = row_to_column(1.0 / (SAMPLES * total))
    secs, count, width = col_ref.shape
    width -= LANES

    def put(at, sums):
        line_ref[:, at] = sums

    column_sums(e_ref, weight_ref, put)
    rows = [line_ref[:, i * width : (i + 1) * width] for i in range(count)]
    tops = jnp.max(top_ref[...], axis=0)
    tops = jnp.concatenate([tops, jnp.zeros((count - tops.shape[0], LANES), F32)], axis=0)
    full = jnp.concatenate([jnp.concatenate(rows, axis=0), tops], axis=1).astype(BF16)
    for i in range(secs):
        col_ref[i] = full


def student_product(
    l_ref, top_ref, w_hbm, send_ref, acc_ref, sum_ref, w_ref, sems
):
    start_stream(w_hbm, w_ref, sems)
    chunk = w_ref.shape[1] // sems.shape[0]
    packed = top_ref[...].astype(BF16).astype(F32)
    top = row_to_column(unpack_row(packed))
    acc_ref[...] = jnp.zeros_like(acc_ref)
    sum_ref[...] = jnp.zeros_like(sum_ref)

    def step(j, carry):
        at = pl.ds(pl.multiple_of(j * chunk, chunk), chunk)
        x = jnp.exp(l_ref[:, at] - tile_lanes(top, chunk // LANES))
        sum_ref[...] += fold_lanes(jnp.add, x)
        wait_stream(w_hbm, w_ref, sems, j)
        acc_ref[...] += lax.dot_general(
            x.astype(BF16), w_ref[:, at], (((1,), (1,)), ((), ())), preferred_element_type=F32
        )
        return carry

    lax.fori_loop(0, sems.shape[0], step, 0)
    high, low = split_high(pack_row(lanes_to_row(sum_ref[...], jnp.sum)))
    write_parts(send_ref, acc_ref[...], [packed, high, low, jnp.zeros_like(low)])


def stack_rows(p1_ref, p2_ref, both_ref):
    low = lax.axis_index("sec") < lax.axis_size("sec") // 2
    half = p1_ref.shape[0]

    @pl.when(low)
    def _():
        both_ref[:half, :] = p1_ref[...]
        both_ref[half:, :] = p2_ref[...]

    @pl.when(jnp.logical_not(low))
    def _():
        both_ref[:half, :] = p2_ref[...]
        both_ref[half:, :] = p1_ref[...]


def crop_first(
    w_hbm, index_ref, both_ref, p3_ref, p4_ref, ec_ref, send_ref, top_ref, crop_ref, rows_ref,
    w_ref, lc_ref, sems,
):
    start_stream(w_hbm, w_ref, sems)
    sec = lax.axis_index("sec")

    @pl.when(jnp.logical_or(sec == 2, sec == 5))
    def _():
        rows_ref[...] = both_ref[...]

    @pl.when(jnp.logical_or(sec == 0, sec == 7))
    def _():
        rows_ref[...] = p3_ref[...]

    @pl.when(jnp.logical_or(sec == 1, sec == 6))
    def _():
        rows_ref[...] = p4_ref[...]

    index = row_to_column(unpack_row(index_ref[...]))
    picked = jnp.zeros(crop_ref.shape, F32)
    for start in range(0, rows_ref.shape[0], 512):
        lane = lax.broadcasted_iota(jnp.int32, (index.shape[0], 512), 1) + start
        hot = jnp.where(tile_lanes(index, 4) == lane, 1.0, 0.0).astype(BF16)
        picked += jnp.dot(hot, rows_ref[start : start + 512, :], preferred_element_type=F32)
    crop_ref[...] = unit_rows(picked)

    def wait(j):
        wait_stream(w_hbm, w_ref, sems, j)

    chunk = w_ref.shape[1] // sems.shape[0]
    logits_into(crop_ref, w_ref, lc_ref, top_ref, 1.0 / TEACH_TEMP, wait, chunk)
    row = lanes_to_row(top_ref[...], jnp.max)
    send_ref[...] = pack_row(row)
    top_ref[...] = row_to_column(row)
    width, block = 512, 64

    def outer(j, carry):
        at = pl.ds(pl.multiple_of(j * width, width), width)

        def inner(i, carry):
            r = pl.ds(pl.multiple_of(i * block, block), block)
            x = jnp.exp(lc_ref[r, at] - tile_lanes(top_ref[r, :], width // LANES))
            ec_ref[r, at] = x.astype(BF16)
            return carry

        return lax.fori_loop(0, lc_ref.shape[0] // block, inner, carry)

    lax.fori_loop(0, lc_ref.shape[1] // width, outer, 0)


def crop_product(
    ec_ref, cols_ref, w_ref, u_ref, index_ref, top_ref, send_ref, c_ref, acc_ref, fix_ref,
    scale_ref, *, chunk=2048,
):
    rows, cols = ec_ref.shape
    _, count, size = cols_ref.shape
    size -= LANES
    first, second = cols_ref[TEACH_A].astype(F32), cols_ref[TEACH_B].astype(F32)
    scale = 1.0 / (PROTOS * (first[:, :size] + second[:, :size]))
    for i in range(count):
        scale_ref[:, i * size : (i + 1) * size] = scale[i : i + 1]
    index = row_to_column(unpack_row(index_ref[...]))
    lane = lax.broadcasted_iota(jnp.int32, index.shape, 1)
    picked = jnp.zeros(index.shape, F32)
    for s, owner in enumerate((first, second)):
        for t in range(rows // LANES):
            tops = owner[t : t + 1, size:]
            picked = jnp.where(index == lane + (s * rows + t * LANES), tops, picked)
    picked = jnp.sum(picked, axis=1, keepdims=True)
    fix_ref[...] = jnp.exp(row_to_column(unpack_row(top_ref[...])) - picked)
    c_ref[...] = jnp.zeros_like(c_ref)
    acc_ref[...] = jnp.zeros_like(acc_ref)

    def step(j, carry):
        at = pl.ds(pl.multiple_of(j * chunk, chunk), chunk)
        y = ec_ref[:, at].astype(F32) * scale_ref[:, at]
        acc_ref[...] += fold_lanes(jnp.add, y)
        c_ref[...] += lax.dot_general(
            y.astype(BF16), w_ref[:, at], (((1,), (1,)), ((), ())), preferred_element_type=F32
        )
        return carry

    lax.fori_loop(0, cols // chunk, step, 0)
    c_ref[...] *= tile_lanes(fix_ref[...], c_ref.shape[1] // LANES)
    cross = fold_lanes(jnp.add, u_ref[...].astype(F32) * c_ref[...]) * (1.0 / STUD_TEMP)
    total = split_high(pack_row(lanes_to_row(acc_ref[...] * fix_ref[...], jnp.sum)))
    cross = split_high(pack_row(lanes_to_row(cross, jnp.sum)))
    write_parts(send_ref, c_ref[...], [*total, *cross])


def finish(a_ref, c_ref, live_ref, grad_ref, loss_ref, weight_ref, stud_ref, targ_ref):
    each, width = grad_ref.shape
    packs = live_ref.shape[0]
    teacher = is_teacher()

    @pl.when(teacher)
    def _():
        grad_ref[...] = jnp.zeros_like(grad_ref)
        loss_ref[...] = jnp.zeros_like(loss_ref)

    @pl.when(jnp.logical_not(teacher))
    def _():
        parts = a_ref.shape[0]
        extra = a_ref[:, :, width:].astype(F32)
        tops = extra[:, :packs]
        top = jnp.max(tops, axis=0)
        weight = jnp.exp(tops - top[None])
        sums = extra[:, packs : 2 * packs] + extra[:, 2 * packs : 3 * packs]
        total = jnp.sum(weight * sums, axis=0)
        rest = jnp.zeros((LANES - parts, LANES), F32)
        for i in range(packs):
            piece = jnp.concatenate([weight[:, i, :], rest], axis=0)
            weight_ref[i * LANES : (i + 1) * LANES, :] = jnp.transpose(piece)
        extra = jnp.sum(c_ref[:, :, width:].astype(F32), axis=0)
        target_sum = extra[:packs] + extra[packs : 2 * packs]
        cross = extra[2 * packs : 3 * packs] + extra[3 * packs :]
        live = live_ref[...].astype(F32)
        loss_ref[...] = live * (top + jnp.log(total) - cross / target_sum)
        scale = live * (1.0 / STUD_TEMP)
        stud_ref[...] = row_to_column(unpack_row(scale / total))
        targ_ref[...] = row_to_column(unpack_row(scale / target_sum))
        mine = pl.ds(pl.multiple_of(lax.axis_index("proto") * each, each), each)
        tiles = width // LANES
        factor = weight_ref[mine, :]
        stud = jnp.zeros(grad_ref.shape, F32)
        for p in range(parts):
            stud += a_ref[p, :, :width].astype(F32) * factor[:, p : p + 1]
        targ = jnp.sum(c_ref[:, :, :width].astype(F32), axis=0)
        grad_ref[...] = stud * tile_lanes(stud_ref[mine, :], tiles) - targ * tile_lanes(
            targ_ref[mine, :], tiles
        )


def fetch(w_hbm, w_ref, sem):
    copy = pltpu.make_async_copy(w_hbm, w_ref, sem)
    copy.start()
    copy.wait()


def hollow(*refs):
    pass


MIB = 2**20
HBM = pltpu.HBM
VMEM = pltpu.VMEM


def call(
    kernel, out, args, scratch=(), alias=None, flops=0, moved=0, limit=8, spaces=None, name=None,
    out_space=VMEM,
):
    spaces = spaces or [VMEM] * len(args)
    return pl.pallas_call(
        kernel,
        name=name or kernel.__name__,
        out_shape=tuple(jax.ShapeDtypeStruct(s, d) for s, d in out),
        in_specs=[pl.BlockSpec(memory_space=s) for s in spaces],
        out_specs=tuple([pl.BlockSpec(memory_space=out_space)] * len(out)),
        scratch_shapes=list(scratch),
        input_output_aliases=alias or {},
        cost_estimate=pl.CostEstimate(flops=flops, bytes_accessed=moved, transcendentals=0),
        compiler_params=pltpu.CompilerParams(vmem_limit_bytes=limit * MIB),
    )(*args)


def per_device(features, prototypes, crop_sample, crop_live):
    rows, width = features.shape
    cols = prototypes.shape[1]
    protos = lax.axis_size("proto")
    secs = lax.axis_size("sec")
    packs = rows // LANES
    each = rows // protos
    row_send = ((protos, packs, LANES), F32)
    one_row = ((packs, LANES), F32)
    parts = ((protos, each, width + LANES), BF16)
    column = ((1, cols), F32)
    columns = ((secs, 8, cols // 8 + LANES), BF16)
    table = ((rows, cols), F32)
    crop_table = ((rows, cols), BF16)
    units = ((rows, width), BF16)
    both_rows = ((2 * rows, width), BF16)
    lanes = VMEM((rows, LANES), F32)
    product = VMEM((rows, width), F32)
    line = VMEM((1, cols), F32)
    protos_vmem = VMEM((width, cols), BF16)
    big = rows * cols * 4
    gemm = 2 * rows * cols * width
    index = crop_sample.reshape(packs, LANES)
    live = crop_live.reshape(packs, LANES)
    pair = [(TEACH_A, TEACH_B), (TEACH_B, TEACH_A)]

    def sems(count):
        return pltpu.SemaphoreType.DMA((count,))

    def spread(x):
        return lax.all_to_all(x, "proto", 0, 0, tiled=True)

    def unused(after, *out):
        return call(hollow, out, [after], spaces=[pl.ANY], out_space=pl.ANY)

    def start(temp, send):
        return call(
            functools.partial(first_logits, scale=1.0 / temp),
            [table, units, send],
            [features, prototypes],
            [lanes, protos_vmem, sems(4)],
            flops=gemm, moved=big, spaces=[VMEM, HBM], limit=32, name="first_logits",
        )

    def teacher(p1):
        logits, _, send = start(TEACH_TEMP, row_send)
        top_got = spread(send)
        expo, col = call(
            teacher_exponentials, [table, column], [logits, top_got], [lanes], {0: 0},
            flops=big, moved=big,
        )
        for last in (False, True):
            peer = lax.ppermute(col, "sec", pair)
            (send,) = call(
                teacher_rows, [row_send], [expo, col, peer], [line, lanes], flops=big, moved=big
            )
            got = spread(send)
            if last:
                (col,) = call(
                    teacher_last, [columns], [expo, got, top_got], [lanes, line], flops=big, moved=big
                )
            else:
                (col,) = call(
                    teacher_columns, [column], [expo, got], [lanes], flops=big, moved=big
                )
        return col, *unused(col, crop_table, crop_table, units, one_row, parts)

    def student(p1):
        p2 = lax.ppermute(p1, "sec", [(2, 5), (5, 2)])
        logits, unit, top = start(STUD_TEMP, one_row)
        top, p2 = lax.optimization_barrier((top, p2))
        (both,) = call(stack_rows, [both_rows], [p1, p2])
        p3 = lax.ppermute(both, "sec", [(2, 0), (5, 7)])
        (send,) = call(
            student_product, [parts], [logits, top, prototypes],
            [product, lanes, protos_vmem, sems(4)],
            flops=gemm, moved=big, spaces=[VMEM, VMEM, HBM], limit=32,
        )
        stud_got = spread(send)
        p3, stud_got = lax.optimization_barrier((p3, stud_got))
        p4 = lax.ppermute(p3, "sec", [(0, 1), (7, 6)])
        crop_expo, crop_top = call(
            crop_first,
            [crop_table, one_row],
            [prototypes, index, both, p3, p4],
            [lanes, VMEM(units[0], BF16), VMEM(both_rows[0], BF16), protos_vmem, VMEM(*table), sems(4)],
            flops=gemm, moved=big, spaces=[HBM] + [VMEM] * 4, limit=36,
        )
        (protos_here,) = call(
            fetch, [crop_table], [prototypes], [pltpu.SemaphoreType.DMA],
            flops=big, moved=big, spaces=[HBM],
        )
        return *unused(crop_expo, columns), crop_expo, protos_here, unit, crop_top, stud_got

    p1 = lax.ppermute(features, "sec", [(3, 2), (4, 5)])
    col, expo, protos_here, unit, crop_top, stud_got = lax.cond(is_teacher(), teacher, student, p1)
    cols_got = lax.all_to_all(col, "sec", 0, 0, tiled=True)
    (send,) = call(
        crop_product,
        [parts],
        [expo, cols_got, protos_here, unit, index, crop_top],
        [product, lanes, lanes, line],
        flops=gemm, moved=big, limit=24,
    )
    grad, loss = call(
        finish,
        [((each, width), F32), ((packs, LANES), F32)],
        [stud_got, spread(send), live],
        [lanes, lanes, lanes],
    )
    return loss.reshape(rows), grad


def solution(mesh):
    in_specs = (P("sec", None), P(None, "proto"), P("sec"), P("sec"))
    out_specs = (P("sec"), P(("sec", "proto"), None))
    return jax.shard_map(
        per_device, mesh=mesh, in_specs=in_specs, out_specs=out_specs, check_vma=False
    )
```

```python
import functools
import math

import jax
import jax.numpy as jnp
from jax import lax
from jax.experimental import pallas as pl
from jax.experimental.pallas import tpu as pltpu
from jax.sharding import PartitionSpec as P

PROTOS = 262144
SAMPLES = 1024
TEACH_TEMP = 0.07
STUD_TEMP = 0.1
TEACH_SCALE = math.log2(math.e) / TEACH_TEMP

F32 = jnp.float32
BF16 = jnp.bfloat16
LANES = 128
SUBS = 8

TEACH_A = 3
TEACH_B = 4

def is_teacher():
    sec = lax.axis_index("sec")
    return jnp.logical_or(sec == TEACH_A, sec == TEACH_B)


def row_to_column(row):
    return jnp.transpose(jnp.broadcast_to(row, (LANES, row.shape[1])))


def lanes_to_row(acc, reduce):
    return reduce(jnp.transpose(acc), axis=0, keepdims=True)


def pack_row(row):
    return jnp.concatenate(
        [row[:, i * LANES : (i + 1) * LANES] for i in range(row.shape[1] // LANES)], axis=0
    )


def unpack_row(packed):
    return jnp.concatenate([packed[i : i + 1, :] for i in range(packed.shape[0])], axis=1)


def tile_lanes(column, count):
    return jnp.concatenate([column] * count, axis=1)


def split_high(x):
    high = x.astype(BF16).astype(F32)
    return high, x - high


def write_parts(send_ref, product, rows):
    parts, each, _ = send_ref.shape
    width = product.shape[1]
    send_ref[:, :, :width] = product.astype(BF16).reshape(parts, each, width)
    extra = jnp.concatenate(rows, axis=0).astype(BF16)
    send_ref[:, :, width:] = jnp.broadcast_to(extra[None], (parts, each, LANES))


def send_copies(ref, packed):
    ref[...] = jnp.broadcast_to(packed[None], ref.shape)


def fold_lanes(op, block):
    out = block[:, :LANES]
    for i in range(1, block.shape[1] // LANES):
        out = op(out, block[:, i * LANES : (i + 1) * LANES])
    return out


def block_copy(w_hbm, w_ref, sems, j):
    chunk = w_ref.shape[1] // sems.shape[0]
    at = pl.ds(pl.multiple_of(j * chunk, chunk), chunk)
    return pltpu.make_async_copy(w_hbm.at[:, at], w_ref.at[:, at], sems.at[j])


def start_stream(w_hbm, w_ref, sems):
    block_copy(w_hbm, w_ref, sems, 0).start()


def wait_stream(w_hbm, w_ref, sems, j):
    block_copy(w_hbm, w_ref, sems, j).wait()

    @pl.when(j + 1 < sems.shape[0])
    def _():
        block_copy(w_hbm, w_ref, sems, j + 1).start()


def unit_rows(features):
    values = features.astype(F32)
    total = jnp.sum(values * values, axis=1, keepdims=True)
    return (values * lax.rsqrt(total + 1e-06)).astype(BF16)


def logits_into(lhs_ref, w_ref, out_ref, top_ref, scale, wait, chunk):
    cols = w_ref.shape[1]
    top_ref[...] = jnp.full(top_ref.shape, -jnp.inf, F32)

    def step(j, carry):
        wait(j)
        at = pl.ds(pl.multiple_of(j * chunk, chunk), chunk)
        z = jnp.dot(lhs_ref[...], w_ref[:, at], preferred_element_type=F32) * scale
        out_ref[:, at] = z
        top_ref[...] = jnp.maximum(top_ref[...], fold_lanes(jnp.maximum, z))
        return carry

    lax.fori_loop(0, cols // chunk, step, 0)


def column_sums(e_ref, weight_ref, put, width=512, block=256):
    rows, cols = e_ref.shape

    def step(j, carry):
        at = pl.ds(pl.multiple_of(j * width, width), width)

        def inner(i, acc):
            r = pl.ds(pl.multiple_of(i * block, block), block)
            x = e_ref[r, at] * tile_lanes(weight_ref[r, :], width // LANES)
            return acc + jnp.sum(x.reshape(block // SUBS, SUBS, width), axis=0)

        acc = lax.fori_loop(0, rows // block, inner, jnp.zeros((SUBS, width), F32))
        put(at, jnp.sum(acc, axis=0, keepdims=True))
        return carry

    lax.fori_loop(0, cols // width, step, 0)


def row_sums(e_ref, scale_ref, acc_ref, block=64, width=1024):
    rows, cols = e_ref.shape

    def step(i, carry):
        r = pl.ds(pl.multiple_of(i * block, block), block)

        def inner(j, acc):
            at = pl.ds(pl.multiple_of(j * width, width), width)
            x = e_ref[r, at] * scale_ref[:, at]
            return acc + fold_lanes(jnp.add, x)

        acc_ref[r, :] = lax.fori_loop(0, cols // width, inner, jnp.zeros((block, LANES), F32))
        return carry

    lax.fori_loop(0, rows // block, step, 0)


def first_logits(x_hbm, w_hbm, l_ref, send_ref, u_ref, x_ref, top_ref, w_ref, x_sem, sems, *, scale):
    copy = pltpu.make_async_copy(x_hbm, x_ref, x_sem)
    copy.start()
    start_stream(w_hbm, w_ref, sems)
    copy.wait()
    u_ref[...] = unit_rows(x_ref[...])

    def wait(j):
        wait_stream(w_hbm, w_ref, sems, j)

    logits_into(u_ref, w_ref, l_ref, top_ref, scale, wait, w_ref.shape[1] // sems.shape[0])
    packed = pack_row(lanes_to_row(top_ref[...], jnp.max))
    if len(send_ref.shape) == 3:
        send_copies(send_ref, packed)
    else:
        send_ref[...] = packed


def teacher_exponentials(l_ref, got_ref, e_ref, col_ref, top_ref, *, width=512, block=256):
    top_ref[...] = row_to_column(unpack_row(jnp.max(got_ref[...], axis=0)))
    rows, cols = e_ref.shape

    def step(j, carry):
        at = pl.ds(pl.multiple_of(j * width, width), width)

        def inner(i, acc):
            r = pl.ds(pl.multiple_of(i * block, block), block)
            x = jnp.exp2(l_ref[r, at] - tile_lanes(top_ref[r, :], width // LANES))
            e_ref[r, at] = x
            return acc + jnp.sum(x.reshape(block // SUBS, SUBS, width), axis=0)

        acc = lax.fori_loop(0, rows // block, inner, jnp.zeros((SUBS, width), F32))
        col_ref[:, at] = jnp.sum(acc, axis=0, keepdims=True)
        return carry

    lax.fori_loop(0, cols // width, step, 0)


def teacher_rows(e_ref, own_ref, peer_ref, send_ref, scale_ref, acc_ref):
    scale_ref[...] = 1.0 / (PROTOS * (own_ref[...] + peer_ref[...]))
    row_sums(e_ref, scale_ref, acc_ref)
    send_copies(send_ref, pack_row(lanes_to_row(acc_ref[...], jnp.sum)))


def teacher_columns(e_ref, got_ref, col_ref, weight_ref):
    total = unpack_row(jnp.sum(got_ref[...], axis=0))
    weight_ref[...] = row_to_column(1.0 / (SAMPLES * total))

    def put(at, sums):
        col_ref[:, at] = sums

    column_sums(e_ref, weight_ref, put)


def teacher_last(e_ref, got_ref, top_ref, col_ref, weight_ref, line_ref):
    total = unpack_row(jnp.sum(got_ref[...], axis=0))
    weight_ref[...] = row_to_column(1.0 / (SAMPLES * total))
    secs, count, width = col_ref.shape
    width -= LANES

    def put(at, sums):
        line_ref[:, at] = sums

    column_sums(e_ref, weight_ref, put)
    rows = [line_ref[:, i * width : (i + 1) * width] for i in range(count)]
    tops = jnp.max(top_ref[...], axis=0)
    tops = jnp.concatenate([tops, jnp.zeros((count - tops.shape[0], LANES), F32)], axis=0)
    full = jnp.concatenate([jnp.concatenate(rows, axis=0), tops], axis=1).astype(BF16)
    for i in range(secs):
        col_ref[i] = full


def student_product(
    l_ref, top_ref, w_hbm, send_ref, acc_ref, sum_ref, w_ref, sems
):
    start_stream(w_hbm, w_ref, sems)
    chunk = w_ref.shape[1] // sems.shape[0]
    packed = top_ref[...].astype(BF16).astype(F32)
    top = row_to_column(unpack_row(packed))
    acc_ref[...] = jnp.zeros_like(acc_ref)
    sum_ref[...] = jnp.zeros_like(sum_ref)

    def step(j, carry):
        at = pl.ds(pl.multiple_of(j * chunk, chunk), chunk)
        x = jnp.exp(l_ref[:, at] - tile_lanes(top, chunk // LANES))
        sum_ref[...] += fold_lanes(jnp.add, x)
        wait_stream(w_hbm, w_ref, sems, j)
        acc_ref[...] += lax.dot_general(
            x.astype(BF16), w_ref[:, at], (((1,), (1,)), ((), ())), preferred_element_type=F32
        )
        return carry

    lax.fori_loop(0, sems.shape[0], step, 0)
    high, low = split_high(pack_row(lanes_to_row(sum_ref[...], jnp.sum)))
    write_parts(send_ref, acc_ref[...], [packed, high, low, jnp.zeros_like(low)])


def stack_rows(p1_ref, p2_ref, both_ref):
    low = lax.axis_index("sec") < lax.axis_size("sec") // 2
    half = p1_ref.shape[0]

    @pl.when(low)
    def _():
        both_ref[:half, :] = p1_ref[...]
        both_ref[half:, :] = p2_ref[...]

    @pl.when(jnp.logical_not(low))
    def _():
        both_ref[:half, :] = p2_ref[...]
        both_ref[half:, :] = p1_ref[...]


def crop_first(
    w_hbm, index_ref, both_ref, p3_ref, p4_ref, ec_ref, send_ref, top_ref, crop_ref, rows_ref,
    w_ref, lc_ref, sems,
):
    start_stream(w_hbm, w_ref, sems)
    sec = lax.axis_index("sec")

    @pl.when(jnp.logical_or(sec == 2, sec == 5))
    def _():
        rows_ref[...] = both_ref[...]

    @pl.when(jnp.logical_or(sec == 0, sec == 7))
    def _():
        rows_ref[...] = p3_ref[...]

    @pl.when(jnp.logical_or(sec == 1, sec == 6))
    def _():
        rows_ref[...] = p4_ref[...]

    index = row_to_column(unpack_row(index_ref[...]))
    picked = jnp.zeros(crop_ref.shape, F32)
    for start in range(0, rows_ref.shape[0], 512):
        lane = lax.broadcasted_iota(jnp.int32, (index.shape[0], 512), 1) + start
        hot = jnp.where(tile_lanes(index, 4) == lane, 1.0, 0.0).astype(BF16)
        picked += jnp.dot(hot, rows_ref[start : start + 512, :], preferred_element_type=F32)
    crop_ref[...] = unit_rows(picked)

    def wait(j):
        wait_stream(w_hbm, w_ref, sems, j)

    chunk = w_ref.shape[1] // sems.shape[0]
    logits_into(crop_ref, w_ref, lc_ref, top_ref, TEACH_SCALE, wait, chunk)
    row = lanes_to_row(top_ref[...], jnp.max)
    send_ref[...] = pack_row(row)
    top_ref[...] = row_to_column(row)
    width, block = 512, 64

    def outer(j, carry):
        at = pl.ds(pl.multiple_of(j * width, width), width)

        def inner(i, carry):
            r = pl.ds(pl.multiple_of(i * block, block), block)
            x = jnp.exp2(lc_ref[r, at] - tile_lanes(top_ref[r, :], width // LANES))
            ec_ref[r, at] = x.astype(BF16)
            return carry

        return lax.fori_loop(0, lc_ref.shape[0] // block, inner, carry)

    lax.fori_loop(0, lc_ref.shape[1] // width, outer, 0)


def crop_product(
    ec_ref, cols_ref, w_ref, u_ref, index_ref, top_ref, send_ref, c_ref, acc_ref, fix_ref,
    scale_ref, *, chunk=2048,
):
    rows, cols = ec_ref.shape
    _, count, size = cols_ref.shape
    size -= LANES
    first, second = cols_ref[TEACH_A].astype(F32), cols_ref[TEACH_B].astype(F32)
    scale = 1.0 / (PROTOS * (first[:, :size] + second[:, :size]))
    for i in range(count):
        scale_ref[:, i * size : (i + 1) * size] = scale[i : i + 1]
    index = row_to_column(unpack_row(index_ref[...]))
    lane = lax.broadcasted_iota(jnp.int32, index.shape, 1)
    picked = jnp.zeros(index.shape, F32)
    for s, owner in enumerate((first, second)):
        for t in range(rows // LANES):
            tops = owner[t : t + 1, size:]
            picked = jnp.where(index == lane + (s * rows + t * LANES), tops, picked)
    picked = jnp.sum(picked, axis=1, keepdims=True)
    fix_ref[...] = jnp.exp2(row_to_column(unpack_row(top_ref[...])) - picked)
    c_ref[...] = jnp.zeros_like(c_ref)
    acc_ref[...] = jnp.zeros_like(acc_ref)

    def step(j, carry):
        at = pl.ds(pl.multiple_of(j * chunk, chunk), chunk)
        y = (ec_ref[:, at].astype(F32) * scale_ref[:, at]).astype(BF16)
        acc_ref[...] += fold_lanes(jnp.add, y.astype(F32))
        c_ref[...] += lax.dot_general(
            y, w_ref[:, at], (((1,), (1,)), ((), ())), preferred_element_type=F32
        )
        return carry

    lax.fori_loop(0, cols // chunk, step, 0)
    c_ref[...] *= tile_lanes(fix_ref[...], c_ref.shape[1] // LANES)
    cross = fold_lanes(jnp.add, u_ref[...].astype(F32) * c_ref[...]) * (1.0 / STUD_TEMP)
    total = split_high(pack_row(lanes_to_row(acc_ref[...] * fix_ref[...], jnp.sum)))
    cross = split_high(pack_row(lanes_to_row(cross, jnp.sum)))
    write_parts(send_ref, c_ref[...], [*total, *cross])


def student_finish(a_ref, live_ref, stud_ref, log_ref, weight_ref, scale_ref):
    each, width = stud_ref.shape
    packs = live_ref.shape[0]
    parts = a_ref.shape[0]
    extra = a_ref[:, :, width:].astype(F32)
    tops = extra[:, :packs]
    top = jnp.max(tops, axis=0)
    weight = jnp.exp(tops - top[None])
    sums = extra[:, packs : 2 * packs] + extra[:, 2 * packs : 3 * packs]
    total = jnp.sum(weight * sums, axis=0)
    log_ref[...] = top + jnp.log(total)
    rest = jnp.zeros((LANES - parts, LANES), F32)
    for i in range(packs):
        piece = jnp.concatenate([weight[:, i, :], rest], axis=0)
        weight_ref[i * LANES : (i + 1) * LANES, :] = jnp.transpose(piece)
    scale = live_ref[...].astype(F32) * (1.0 / STUD_TEMP) / total
    scale_ref[...] = row_to_column(unpack_row(scale))
    mine = pl.ds(pl.multiple_of(lax.axis_index("proto") * each, each), each)
    factor = weight_ref[mine, :]
    stud = jnp.zeros(stud_ref.shape, F32)
    for p in range(parts):
        stud += a_ref[p, :, :width].astype(F32) * factor[:, p : p + 1]
    stud_ref[...] = stud * tile_lanes(scale_ref[mine, :], width // LANES)


def finish(stud_ref, log_ref, c_ref, live_ref, grad_ref, loss_ref, scale_ref):
    each, width = grad_ref.shape
    packs = live_ref.shape[0]
    teacher = is_teacher()

    @pl.when(teacher)
    def _():
        grad_ref[...] = jnp.zeros_like(grad_ref)
        loss_ref[...] = jnp.zeros_like(loss_ref)

    @pl.when(jnp.logical_not(teacher))
    def _():
        extra = jnp.sum(c_ref[:, :, width:].astype(F32), axis=0)
        target_sum = extra[:packs] + extra[packs : 2 * packs]
        cross = extra[2 * packs : 3 * packs] + extra[3 * packs :]
        live = live_ref[...].astype(F32)
        loss_ref[...] = live * (log_ref[...] - cross / target_sum)
        scale_ref[...] = row_to_column(unpack_row(live * (1.0 / STUD_TEMP) / target_sum))
        mine = pl.ds(pl.multiple_of(lax.axis_index("proto") * each, each), each)
        targ = jnp.sum(c_ref[:, :, :width].astype(F32), axis=0)
        grad_ref[...] = stud_ref[...] - targ * tile_lanes(scale_ref[mine, :], width // LANES)


def fetch(w_hbm, w_ref, sem):
    copy = pltpu.make_async_copy(w_hbm, w_ref, sem)
    copy.start()
    copy.wait()


def hollow(*refs):
    pass


MIB = 2**20
HBM = pltpu.HBM
VMEM = pltpu.VMEM


def call(
    kernel, out, args, scratch=(), alias=None, flops=0, moved=0, limit=8, spaces=None, name=None,
    out_space=VMEM,
):
    spaces = spaces or [VMEM] * len(args)
    return pl.pallas_call(
        kernel,
        name=name or kernel.__name__,
        out_shape=tuple(jax.ShapeDtypeStruct(s, d) for s, d in out),
        in_specs=[pl.BlockSpec(memory_space=s) for s in spaces],
        out_specs=tuple([pl.BlockSpec(memory_space=out_space)] * len(out)),
        scratch_shapes=list(scratch),
        input_output_aliases=alias or {},
        cost_estimate=pl.CostEstimate(flops=flops, bytes_accessed=moved, transcendentals=0),
        compiler_params=pltpu.CompilerParams(vmem_limit_bytes=limit * MIB),
    )(*args)


def per_device(features, prototypes, crop_sample, crop_live):
    rows, width = features.shape
    cols = prototypes.shape[1]
    protos = lax.axis_size("proto")
    secs = lax.axis_size("sec")
    packs = rows // LANES
    each = rows // protos
    row_send = ((protos, packs, LANES), F32)
    one_row = ((packs, LANES), F32)
    parts = ((protos, each, width + LANES), BF16)
    part_rows = ((each, width), F32)
    column = ((1, cols), F32)
    columns = ((secs, 8, cols // 8 + LANES), BF16)
    table = ((rows, cols), F32)
    crop_table = ((rows, cols), BF16)
    units = ((rows, width), BF16)
    both_rows = ((2 * rows, width), BF16)
    lanes = VMEM((rows, LANES), F32)
    product = VMEM((rows, width), F32)
    line = VMEM((1, cols), F32)
    protos_vmem = VMEM((width, cols), BF16)
    big = rows * cols * 4
    gemm = 2 * rows * cols * width
    index = crop_sample.reshape(packs, LANES)
    live = crop_live.reshape(packs, LANES)
    pair = [(TEACH_A, TEACH_B), (TEACH_B, TEACH_A)]

    def sems(count):
        return pltpu.SemaphoreType.DMA((count,))

    def spread(x):
        return lax.all_to_all(x, "proto", 0, 0, tiled=True)

    def unused(after, *out):
        return call(hollow, out, [after], spaces=[pl.ANY], out_space=pl.ANY)

    def start(scale, send, keep):
        unit = VMEM(*units)
        return call(
            functools.partial(first_logits, scale=scale),
            [table, send, units] if keep else [table, send],
            [features, prototypes],
            [
                *([] if keep else [unit]), unit, lanes, protos_vmem,
                pltpu.SemaphoreType.DMA, sems(4),
            ],
            flops=gemm, moved=big, spaces=[HBM, HBM], limit=32, name="first_logits",
        )

    def teacher(p1):
        logits, send = start(TEACH_SCALE, row_send, False)
        top_got = spread(send)
        expo, col = call(
            teacher_exponentials, [table, column], [logits, top_got], [lanes], {0: 0},
            flops=big, moved=big,
        )
        for last in (False, True):
            peer = lax.ppermute(col, "sec", pair)
            (send,) = call(
                teacher_rows, [row_send], [expo, col, peer], [line, lanes], flops=big, moved=big
            )
            got = spread(send)
            if last:
                (col,) = call(
                    teacher_last, [columns], [expo, got, top_got], [lanes, line], flops=big, moved=big
                )
            else:
                (col,) = call(
                    teacher_columns, [column], [expo, got], [lanes], flops=big, moved=big
                )
        return col, *unused(
            col, crop_table, crop_table, units, one_row, part_rows, one_row
        )

    def student(p1):
        p2 = lax.ppermute(p1, "sec", [(2, 5), (5, 2)])
        logits, top, unit = start(1.0 / STUD_TEMP, one_row, True)
        top, p2 = lax.optimization_barrier((top, p2))
        (both,) = call(stack_rows, [both_rows], [p1, p2])
        p3 = lax.ppermute(both, "sec", [(2, 0), (5, 7)])
        (send,) = call(
            student_product, [parts], [logits, top, prototypes],
            [product, lanes, protos_vmem, sems(4)],
            flops=gemm, moved=big, spaces=[VMEM, VMEM, HBM], limit=32,
        )
        stud_got = spread(send)
        p3, stud_got = lax.optimization_barrier((p3, stud_got))
        p4 = lax.ppermute(p3, "sec", [(0, 1), (7, 6)])
        crop_expo, crop_top = call(
            crop_first,
            [crop_table, one_row],
            [prototypes, index, both, p3, p4],
            [lanes, VMEM(units[0], BF16), VMEM(both_rows[0], BF16), protos_vmem, VMEM(*table), sems(4)],
            flops=gemm, moved=big, spaces=[HBM] + [VMEM] * 4, limit=36,
        )
        (protos_here,) = call(
            fetch, [crop_table], [prototypes], [pltpu.SemaphoreType.DMA],
            flops=big, moved=big, spaces=[HBM],
        )
        stud, log_total = call(
            student_finish, [part_rows, one_row], [stud_got, live], [lanes, lanes]
        )
        return *unused(crop_expo, columns), crop_expo, protos_here, unit, crop_top, stud, log_total

    p1 = lax.ppermute(features, "sec", [(3, 2), (4, 5)])
    col, expo, protos_here, unit, crop_top, stud, log_total = lax.cond(
        is_teacher(), teacher, student, p1
    )
    cols_got = lax.all_to_all(col, "sec", 0, 0, tiled=True)
    (send,) = call(
        crop_product,
        [parts],
        [expo, cols_got, protos_here, unit, index, crop_top],
        [product, lanes, lanes, line],
        flops=gemm, moved=big, limit=24,
    )
    grad, loss = call(
        finish,
        [part_rows, one_row],
        [stud, log_total, spread(send), live],
        [lanes],
    )
    return loss.reshape(rows), grad


def solution(mesh):
    in_specs = (P("sec", None), P(None, "proto"), P("sec"), P("sec"))
    out_specs = (P("sec"), P(("sec", "proto"), None))
    return jax.shard_map(
        per_device, mesh=mesh, in_specs=in_specs, out_specs=out_specs, check_vma=False
    )
```

```python
import functools
import math

import jax
import jax.numpy as jnp
from jax import lax
from jax.experimental import pallas as pl
from jax.experimental.pallas import tpu as pltpu
from jax.sharding import PartitionSpec as P


PROTOS = 262144
SAMPLES = 1024
TEACH_TEMP = 0.07
STUD_TEMP = 0.1
TEACH_SCALE = math.log2(math.e) / TEACH_TEMP

F32 = jnp.float32
BF16 = jnp.bfloat16
LANES = 128
SUBS = 8

TEACH_A = 3
TEACH_B = 4


def is_teacher():
    sec = lax.axis_index("sec")
    return jnp.logical_or(sec == TEACH_A, sec == TEACH_B)


def row_to_column(row):
    return jnp.transpose(jnp.broadcast_to(row, (LANES, row.shape[1])))


def lanes_to_row(acc, reduce):
    return reduce(jnp.transpose(acc), axis=0, keepdims=True)


def pack_row(row):
    return jnp.concatenate(
        [row[:, i * LANES : (i + 1) * LANES] for i in range(row.shape[1] // LANES)], axis=0
    )


def unpack_row(packed):
    return jnp.concatenate([packed[i : i + 1, :] for i in range(packed.shape[0])], axis=1)


def tile_lanes(column, count):
    return jnp.concatenate([column] * count, axis=1)


def split_high(x):
    high = x.astype(BF16).astype(F32)
    return high, x - high


def write_parts(send_ref, product, rows):
    parts, each, _ = send_ref.shape
    width = product.shape[1]
    send_ref[:, :, :width] = product.astype(BF16).reshape(parts, each, width)
    extra = jnp.concatenate(rows, axis=0).astype(BF16)
    send_ref[:, :, width:] = jnp.broadcast_to(extra[None], (parts, each, LANES))


def send_copies(ref, packed):
    ref[...] = jnp.broadcast_to(packed[None], ref.shape)


def fold_lanes(op, block):
    out = block[:, :LANES]
    for i in range(1, block.shape[1] // LANES):
        out = op(out, block[:, i * LANES : (i + 1) * LANES])
    return out


def block_copy(w_hbm, w_ref, sems, j):
    chunk = w_ref.shape[1] // sems.shape[0]
    at = pl.ds(pl.multiple_of(j * chunk, chunk), chunk)
    return pltpu.make_async_copy(w_hbm.at[:, at], w_ref.at[:, at], sems.at[j])


def start_stream(w_hbm, w_ref, sems):
    block_copy(w_hbm, w_ref, sems, 0).start()


def wait_stream(w_hbm, w_ref, sems, j):
    block_copy(w_hbm, w_ref, sems, j).wait()

    @pl.when(j + 1 < sems.shape[0])
    def _():
        block_copy(w_hbm, w_ref, sems, j + 1).start()


def unit_rows(features):
    values = features.astype(F32)
    total = jnp.sum(values * values, axis=1, keepdims=True)
    return (values * lax.rsqrt(total + 1e-06)).astype(BF16)


def logits_into(lhs_ref, w_ref, out_ref, top_ref, scale, wait, chunk):
    cols = w_ref.shape[1]
    top_ref[...] = jnp.full(top_ref.shape, -jnp.inf, F32)

    def step(j, carry):
        wait(j)
        at = pl.ds(pl.multiple_of(j * chunk, chunk), chunk)
        z = jnp.dot(lhs_ref[...], w_ref[:, at], preferred_element_type=F32) * scale
        out_ref[:, at] = z
        top_ref[...] = jnp.maximum(top_ref[...], fold_lanes(jnp.maximum, z))
        return carry

    lax.fori_loop(0, cols // chunk, step, 0)


def column_sums(e_ref, weight_ref, put, width=512, block=256):
    rows, cols = e_ref.shape

    def step(j, carry):
        at = pl.ds(pl.multiple_of(j * width, width), width)

        def inner(i, acc):
            r = pl.ds(pl.multiple_of(i * block, block), block)
            x = e_ref[r, at] * tile_lanes(weight_ref[r, :], width // LANES)
            return acc + jnp.sum(x.reshape(block // SUBS, SUBS, width), axis=0)

        acc = lax.fori_loop(0, rows // block, inner, jnp.zeros((SUBS, width), F32))
        put(at, jnp.sum(acc, axis=0, keepdims=True))
        return carry

    lax.fori_loop(0, cols // width, step, 0)


def row_sums(e_ref, scale_ref, acc_ref, block=64, width=1024):
    rows, cols = e_ref.shape

    def step(i, carry):
        r = pl.ds(pl.multiple_of(i * block, block), block)

        def inner(j, acc):
            at = pl.ds(pl.multiple_of(j * width, width), width)
            x = e_ref[r, at] * scale_ref[:, at]
            return acc + fold_lanes(jnp.add, x)

        acc_ref[r, :] = lax.fori_loop(0, cols // width, inner, jnp.zeros((block, LANES), F32))
        return carry

    lax.fori_loop(0, rows // block, step, 0)


def first_logits(x_hbm, w_hbm, l_ref, send_ref, u_ref, x_ref, top_ref, w_ref, x_sem, sems, *, scale):
    copy = pltpu.make_async_copy(x_hbm, x_ref, x_sem)
    copy.start()
    start_stream(w_hbm, w_ref, sems)
    copy.wait()
    u_ref[...] = unit_rows(x_ref[...])

    def wait(j):
        wait_stream(w_hbm, w_ref, sems, j)

    logits_into(u_ref, w_ref, l_ref, top_ref, scale, wait, w_ref.shape[1] // sems.shape[0])
    packed = pack_row(lanes_to_row(top_ref[...], jnp.max))
    if len(send_ref.shape) == 3:
        send_copies(send_ref, packed)
    else:
        send_ref[...] = packed


def teacher_exponentials(l_ref, got_ref, e_ref, col_ref, top_ref, *, width=512, block=256):
    top_ref[...] = row_to_column(unpack_row(jnp.max(got_ref[...], axis=0)))
    rows, cols = e_ref.shape

    def step(j, carry):
        at = pl.ds(pl.multiple_of(j * width, width), width)

        def inner(i, acc):
            r = pl.ds(pl.multiple_of(i * block, block), block)
            x = jnp.exp2(l_ref[r, at] - tile_lanes(top_ref[r, :], width // LANES))
            e_ref[r, at] = x
            return acc + jnp.sum(x.reshape(block // SUBS, SUBS, width), axis=0)

        acc = lax.fori_loop(0, rows // block, inner, jnp.zeros((SUBS, width), F32))
        col_ref[:, at] = jnp.sum(acc, axis=0, keepdims=True)
        return carry

    lax.fori_loop(0, cols // width, step, 0)


def teacher_rows(e_ref, own_ref, peer_ref, send_ref, scale_ref, acc_ref):
    scale_ref[...] = 1.0 / (PROTOS * (own_ref[...] + peer_ref[...]))
    row_sums(e_ref, scale_ref, acc_ref)
    send_copies(send_ref, pack_row(lanes_to_row(acc_ref[...], jnp.sum)))


def teacher_columns(e_ref, got_ref, col_ref, weight_ref):
    total = unpack_row(jnp.sum(got_ref[...], axis=0))
    weight_ref[...] = row_to_column(1.0 / (SAMPLES * total))

    def put(at, sums):
        col_ref[:, at] = sums

    column_sums(e_ref, weight_ref, put)


def teacher_last(e_ref, got_ref, top_ref, col_ref, weight_ref, line_ref):
    total = unpack_row(jnp.sum(got_ref[...], axis=0))
    weight_ref[...] = row_to_column(1.0 / (SAMPLES * total))
    secs, count, width = col_ref.shape
    width -= LANES

    def put(at, sums):
        line_ref[:, at] = sums

    column_sums(e_ref, weight_ref, put)
    rows = [line_ref[:, i * width : (i + 1) * width] for i in range(count)]
    tops = jnp.max(top_ref[...], axis=0)
    tops = jnp.concatenate([tops, jnp.zeros((count - tops.shape[0], LANES), F32)], axis=0)
    full = jnp.concatenate([jnp.concatenate(rows, axis=0), tops], axis=1).astype(BF16)
    for i in range(secs):
        col_ref[i] = full


def student_product(
    l_ref, top_ref, w_hbm, send_ref, acc_ref, sum_ref, w_ref, sems
):
    start_stream(w_hbm, w_ref, sems)
    chunk = w_ref.shape[1] // sems.shape[0]
    packed = top_ref[...].astype(BF16).astype(F32)
    top = row_to_column(unpack_row(packed))
    acc_ref[...] = jnp.zeros_like(acc_ref)
    sum_ref[...] = jnp.zeros_like(sum_ref)

    def step(j, carry):
        at = pl.ds(pl.multiple_of(j * chunk, chunk), chunk)
        x = jnp.exp(l_ref[:, at] - tile_lanes(top, chunk // LANES))
        sum_ref[...] += fold_lanes(jnp.add, x)
        wait_stream(w_hbm, w_ref, sems, j)
        acc_ref[...] += lax.dot_general(
            x.astype(BF16), w_ref[:, at], (((1,), (1,)), ((), ())), preferred_element_type=F32
        )
        return carry

    lax.fori_loop(0, sems.shape[0], step, 0)
    high, low = split_high(pack_row(lanes_to_row(sum_ref[...], jnp.sum)))
    write_parts(send_ref, acc_ref[...], [packed, high, low, jnp.zeros_like(low)])


def pick_rows(p1_ref, p0_ref, rows_ref):
    near = lax.axis_index("proto") < lax.axis_size("proto") // 2

    @pl.when(near)
    def _():
        rows_ref[...] = p1_ref[...]

    @pl.when(jnp.logical_not(near))
    def _():
        rows_ref[...] = p0_ref[...]


def stack_rows(p1_ref, p2_ref, both_ref):
    low = lax.axis_index("sec") < lax.axis_size("sec") // 2
    half = p1_ref.shape[0]

    @pl.when(low)
    def _():
        both_ref[:half, :] = p1_ref[...]
        both_ref[half:, :] = p2_ref[...]

    @pl.when(jnp.logical_not(low))
    def _():
        both_ref[:half, :] = p2_ref[...]
        both_ref[half:, :] = p1_ref[...]


def crop_first(
    w_hbm, index_ref, both_ref, p3_ref, p4_ref, ec_ref, send_ref, top_ref, crop_ref, rows_ref,
    w_ref, lc_ref, sems,
):
    start_stream(w_hbm, w_ref, sems)
    sec = lax.axis_index("sec")

    @pl.when(jnp.logical_or(sec == 2, sec == 5))
    def _():
        rows_ref[...] = both_ref[...]

    @pl.when(jnp.logical_or(sec == 0, sec == 7))
    def _():
        rows_ref[...] = p3_ref[...]

    @pl.when(jnp.logical_or(sec == 1, sec == 6))
    def _():
        rows_ref[...] = p4_ref[...]

    index = row_to_column(unpack_row(index_ref[...]))
    picked = jnp.zeros(crop_ref.shape, F32)
    for start in range(0, rows_ref.shape[0], 512):
        lane = lax.broadcasted_iota(jnp.int32, (index.shape[0], 512), 1) + start
        hot = jnp.where(tile_lanes(index, 4) == lane, 1.0, 0.0).astype(BF16)
        picked += jnp.dot(hot, rows_ref[start : start + 512, :], preferred_element_type=F32)
    crop_ref[...] = unit_rows(picked)

    def wait(j):
        wait_stream(w_hbm, w_ref, sems, j)

    chunk = w_ref.shape[1] // sems.shape[0]
    logits_into(crop_ref, w_ref, lc_ref, top_ref, TEACH_SCALE, wait, chunk)
    row = lanes_to_row(top_ref[...], jnp.max)
    send_ref[...] = pack_row(row)
    top_ref[...] = row_to_column(row)
    width, block = 512, 64

    def outer(j, carry):
        at = pl.ds(pl.multiple_of(j * width, width), width)

        def inner(i, carry):
            r = pl.ds(pl.multiple_of(i * block, block), block)
            x = jnp.exp2(lc_ref[r, at] - tile_lanes(top_ref[r, :], width // LANES))
            ec_ref[r, at] = x.astype(BF16)
            return carry

        return lax.fori_loop(0, lc_ref.shape[0] // block, inner, carry)

    lax.fori_loop(0, lc_ref.shape[1] // width, outer, 0)


def crop_product(
    ec_ref, cols_ref, w_ref, u_ref, index_ref, top_ref, send_ref, c_ref, acc_ref, fix_ref,
    scale_ref, *, chunk=2048,
):
    rows, cols = ec_ref.shape
    _, count, size = cols_ref.shape
    size -= LANES
    first, second = cols_ref[TEACH_A].astype(F32), cols_ref[TEACH_B].astype(F32)
    scale = 1.0 / (PROTOS * (first[:, :size] + second[:, :size]))
    for i in range(count):
        scale_ref[:, i * size : (i + 1) * size] = scale[i : i + 1]
    index = row_to_column(unpack_row(index_ref[...]))
    lane = lax.broadcasted_iota(jnp.int32, index.shape, 1)
    picked = jnp.zeros(index.shape, F32)
    for s, owner in enumerate((first, second)):
        for t in range(rows // LANES):
            tops = owner[t : t + 1, size:]
            picked = jnp.where(index == lane + (s * rows + t * LANES), tops, picked)
    picked = jnp.sum(picked, axis=1, keepdims=True)
    fix_ref[...] = jnp.exp2(row_to_column(unpack_row(top_ref[...])) - picked)
    c_ref[...] = jnp.zeros_like(c_ref)
    acc_ref[...] = jnp.zeros_like(acc_ref)

    def step(j, carry):
        at = pl.ds(pl.multiple_of(j * chunk, chunk), chunk)
        y = (ec_ref[:, at].astype(F32) * scale_ref[:, at]).astype(BF16)
        acc_ref[...] += fold_lanes(jnp.add, y.astype(F32))
        c_ref[...] += lax.dot_general(
            y, w_ref[:, at], (((1,), (1,)), ((), ())), preferred_element_type=F32
        )
        return carry

    lax.fori_loop(0, cols // chunk, step, 0)
    c_ref[...] *= tile_lanes(fix_ref[...], c_ref.shape[1] // LANES)
    cross = fold_lanes(jnp.add, u_ref[...].astype(F32) * c_ref[...]) * (1.0 / STUD_TEMP)
    total = split_high(pack_row(lanes_to_row(acc_ref[...] * fix_ref[...], jnp.sum)))
    cross = split_high(pack_row(lanes_to_row(cross, jnp.sum)))
    write_parts(send_ref, c_ref[...], [*total, *cross])


def student_finish(a_ref, live_ref, stud_ref, log_ref, weight_ref, scale_ref):
    each, width = stud_ref.shape
    packs = live_ref.shape[0]
    parts = a_ref.shape[0]
    extra = a_ref[:, :, width:].astype(F32)
    tops = extra[:, :packs]
    top = jnp.max(tops, axis=0)
    weight = jnp.exp(tops - top[None])
    sums = extra[:, packs : 2 * packs] + extra[:, 2 * packs : 3 * packs]
    total = jnp.sum(weight * sums, axis=0)
    log_ref[...] = top + jnp.log(total)
    rest = jnp.zeros((LANES - parts, LANES), F32)
    for i in range(packs):
        piece = jnp.concatenate([weight[:, i, :], rest], axis=0)
        weight_ref[i * LANES : (i + 1) * LANES, :] = jnp.transpose(piece)
    scale = live_ref[...].astype(F32) * (1.0 / STUD_TEMP) / total
    scale_ref[...] = row_to_column(unpack_row(scale))
    mine = pl.ds(pl.multiple_of(lax.axis_index("proto") * each, each), each)
    factor = weight_ref[mine, :]
    stud = jnp.zeros(stud_ref.shape, F32)
    for p in range(parts):
        stud += a_ref[p, :, :width].astype(F32) * factor[:, p : p + 1]
    stud_ref[...] = stud * tile_lanes(scale_ref[mine, :], width // LANES)


def finish(stud_ref, log_ref, c_ref, live_ref, grad_ref, loss_ref, scale_ref):
    each, width = grad_ref.shape
    packs = live_ref.shape[0]
    teacher = is_teacher()

    @pl.when(teacher)
    def _():
        grad_ref[...] = jnp.zeros_like(grad_ref)
        loss_ref[...] = jnp.zeros_like(loss_ref)

    @pl.when(jnp.logical_not(teacher))
    def _():
        extra = jnp.sum(c_ref[:, :, width:].astype(F32), axis=0)
        target_sum = extra[:packs] + extra[packs : 2 * packs]
        cross = extra[2 * packs : 3 * packs] + extra[3 * packs :]
        live = live_ref[...].astype(F32)
        loss_ref[...] = live * (log_ref[...] - cross / target_sum)
        scale_ref[...] = row_to_column(unpack_row(live * (1.0 / STUD_TEMP) / target_sum))
        mine = pl.ds(pl.multiple_of(lax.axis_index("proto") * each, each), each)
        targ = jnp.sum(c_ref[:, :, :width].astype(F32), axis=0)
        grad_ref[...] = stud_ref[...] - targ * tile_lanes(scale_ref[mine, :], width // LANES)


def fetch(w_hbm, w_ref, sem):
    copy = pltpu.make_async_copy(w_hbm, w_ref, sem)
    copy.start()
    copy.wait()


def hollow(*refs):
    pass


MIB = 2**20
HBM = pltpu.HBM
VMEM = pltpu.VMEM


def call(
    kernel, out, args, scratch=(), alias=None, flops=0, moved=0, limit=8, spaces=None,
    out_space=VMEM,
):
    spaces = spaces or [VMEM] * len(args)
    return pl.pallas_call(
        kernel,
        out_shape=tuple(jax.ShapeDtypeStruct(s, d) for s, d in out),
        in_specs=[pl.BlockSpec(memory_space=s) for s in spaces],
        out_specs=tuple([pl.BlockSpec(memory_space=out_space)] * len(out)),
        scratch_shapes=list(scratch),
        input_output_aliases=alias or {},
        cost_estimate=pl.CostEstimate(flops=flops, bytes_accessed=moved, transcendentals=0),
        compiler_params=pltpu.CompilerParams(vmem_limit_bytes=limit * MIB),
    )(*args)


def per_device(features, prototypes, crop_sample, crop_live):
    rows, width = features.shape
    cols = prototypes.shape[1]
    protos = lax.axis_size("proto")
    secs = lax.axis_size("sec")
    packs = rows // LANES
    each = rows // protos
    row_send = ((protos, packs, LANES), F32)
    one_row = ((packs, LANES), F32)
    parts = ((protos, each, width + LANES), BF16)
    part_rows = ((each, width), F32)
    column = ((1, cols), F32)
    columns = ((secs, 8, cols // 8 + LANES), BF16)
    table = ((rows, cols), F32)
    crop_table = ((rows, cols), BF16)
    units = ((rows, width), BF16)
    both_rows = ((2 * rows, width), BF16)
    lanes = VMEM((rows, LANES), F32)
    product = VMEM((rows, width), F32)
    line = VMEM((1, cols), F32)
    protos_vmem = VMEM((width, cols), BF16)
    big = rows * cols * 4
    gemm = 2 * rows * cols * width
    index = crop_sample.reshape(packs, LANES)
    live = crop_live.reshape(packs, LANES)
    pair = [(TEACH_A, TEACH_B), (TEACH_B, TEACH_A)]

    def sems(count):
        return pltpu.SemaphoreType.DMA((count,))

    def spread(x):
        return lax.all_to_all(x, "proto", 0, 0, tiled=True)

    def unused(after, *out):
        return call(hollow, out, [after], spaces=[pl.ANY], out_space=pl.ANY)

    def start(scale, send, keep):
        unit = VMEM(*units)
        return call(
            functools.partial(first_logits, scale=scale),
            [table, send, units] if keep else [table, send],
            [features, prototypes],
            [
                *([] if keep else [unit]), unit, lanes, protos_vmem,
                pltpu.SemaphoreType.DMA, sems(4),
            ],
            flops=gemm, moved=big, spaces=[HBM, HBM], limit=32,
        )

    def teacher(p1):
        logits, send = start(TEACH_SCALE, row_send, False)
        top_got = spread(send)
        expo, col = call(
            teacher_exponentials, [table, column], [logits, top_got], [lanes], {0: 0},
            flops=big, moved=big,
        )
        for last in (False, True):
            peer = lax.ppermute(col, "sec", pair)
            (send,) = call(
                teacher_rows, [row_send], [expo, col, peer], [line, lanes], flops=big, moved=big
            )
            got = spread(send)
            if last:
                (col,) = call(
                    teacher_last, [columns], [expo, got, top_got], [lanes, line], flops=big, moved=big
                )
            else:
                (col,) = call(
                    teacher_columns, [column], [expo, got], [lanes], flops=big, moved=big
                )
        return col, *unused(
            col, crop_table, crop_table, units, one_row, part_rows, one_row
        )

    def student(p1):
        across = [(s * protos + p, s * protos + p + half) for s in (2, 5) for p in range(half)]
        p0 = lax.ppermute(p1, ("sec", "proto"), across)
        logits, top, unit = start(1.0 / STUD_TEMP, one_row, True)
        top, p0 = lax.optimization_barrier((top, p0))
        (rows_here,) = call(pick_rows, [units], [p1, p0])
        p2 = lax.ppermute(rows_here, "sec", [(2, 5), (5, 2)])
        (both,) = call(stack_rows, [both_rows], [rows_here, p2])
        top, both = lax.optimization_barrier((top, both))
        p3 = lax.ppermute(both, "sec", [(2, 0), (5, 7)])
        (send,) = call(
            student_product, [parts], [logits, top, prototypes],
            [product, lanes, protos_vmem, sems(4)],
            flops=gemm, moved=big, spaces=[VMEM, VMEM, HBM], limit=32,
        )
        stud_got = spread(send)
        p3, stud_got = lax.optimization_barrier((p3, stud_got))
        p4 = lax.ppermute(p3, "sec", [(0, 1), (7, 6)])
        crop_expo, crop_top = call(
            crop_first,
            [crop_table, one_row],
            [prototypes, index, both, p3, p4],
            [lanes, VMEM(units[0], BF16), VMEM(both_rows[0], BF16), protos_vmem, VMEM(*table), sems(4)],
            flops=gemm, moved=big, spaces=[HBM] + [VMEM] * 4, limit=36,
        )
        (protos_here,) = call(
            fetch, [crop_table], [prototypes], [pltpu.SemaphoreType.DMA],
            flops=big, moved=big, spaces=[HBM],
        )
        stud, log_total = call(
            student_finish, [part_rows, one_row], [stud_got, live], [lanes, lanes]
        )
        return *unused(crop_expo, columns), crop_expo, protos_here, unit, crop_top, stud, log_total

    half = protos // 2
    moves = [(3 * protos + p, 2 * protos + p) for p in range(half)]
    moves += [(4 * protos + p, 5 * protos + p) for p in range(half)]
    p1 = lax.ppermute(features, ("sec", "proto"), moves)
    col, expo, protos_here, unit, crop_top, stud, log_total = lax.cond(
        is_teacher(), teacher, student, p1
    )
    cols_got = lax.all_to_all(col, "sec", 0, 0, tiled=True)
    (send,) = call(
        crop_product,
        [parts],
        [expo, cols_got, protos_here, unit, index, crop_top],
        [product, lanes, lanes, line],
        flops=gemm, moved=big, limit=24,
    )
    grad, loss = call(
        finish,
        [part_rows, one_row],
        [stud, log_total, spread(send), live],
        [lanes],
    )
    return loss.reshape(rows), grad


def solution(mesh):
    in_specs = (P("sec", None), P(None, "proto"), P("sec"), P("sec"))
    out_specs = (P("sec"), P(("sec", "proto"), None))
    return jax.shard_map(
        per_device, mesh=mesh, in_specs=in_specs, out_specs=out_specs, check_vma=False
    )
```
